32 devices in a mesh: groups: 2 (over y), blk: 4 (over z), col: 4 (over x, core).
Axes of the slice: x: 2, y: 2, z: 4, core: 2. Of those that a mesh axis runs over, the one named last changes fastest.
Arguments:
- aic: float32 [256, 32768], P(('groups', 'blk'), 'col'), parts along dimension 0, may hold values from -0.03125 to 0.03125
- downwash: float32 [8, 8192, 384], P(('groups', 'col'), 'blk'), parts along dimension 0, may hold values from -6 to 6
- node_modes: float32 [6, 32, 192], P(None, 'blk'), may hold values from -0.4375 to 0.4375
- src_rows: int32 [4, 4, 4, 8], P('blk', 'col'), may hold values from 0 to 7
- dst_nodes: int32 [4, 4, 4, 8], P('blk', 'col'), may hold values from 0 to 7
- counts: int32 [4, 4, 4], P('blk', 'col'), may hold values from 0 to 8, as said below
- spline_weights: float32 [4, 4, 6, 4, 8], P('blk', 'col'), may hold values from -0.6 to 0.6
Outputs:
- gaf: float32 [384, 384], P('groups'), parts along dimension 0
The draws below stay inside these ranges and needn't reach their ends.
There are 2 independent parts, one for each index of `groups`. The reference program is written for one: setup_inputs(seed, part) draws one part's arguments, and reference() takes and returns one part's arrays. A program takes and returns all parts, laid end to end along the dimension named above; an argument that names none is the same for every part. Nothing has to cross between parts.
Inputs may be any that keep to these rules, and one draw needn't show every extreme that they name: `counts`: slot s of a list is live when s < count; every source sub-block sends 8 live slots to its own owner, and one owner receives 8 live slots from every source sub-block. `src_rows`: rows within a sub-block of 8 rows. `dst_nodes`: nodes within an owner.
All inputs are finite; a program needn't handle non-finite values.
Results may differ from the reference program's by a relative error of at most 0.0003.
Values sent between devices are 32-bit elements; how exact they have to be, the bound alone decides.
A program may use at most 64 MiB of HBM per device.

```python
import jax
import jax.numpy as jnp
from jax import lax

PANELS = 32768
MODES = 192
ROW_DEV = 32
CAP = 8
NODE_DEV = 8
ROWS = 128
PCOL = 8192
ROW_SUB = 8
NODES = 32
N_BLK = 4
N_COL = 4


def draw_counts(key, part):
    key_level = jax.random.fold_in(key, 11)
    key_count = jax.random.fold_in(key, 12)
    key_star = jax.random.fold_in(key, 13)
    level = jax.random.randint(key_level, (N_BLK,), 0, 3)
    limit = CAP * (2 + level) // 4
    drawn = jax.random.randint(key_count, (N_BLK, N_COL, N_BLK), 0, limit[None, None, :] + 1)
    star = jax.random.randint(key_star, (), 0, N_BLK)
    owner = jnp.arange(N_BLK)[None, None, :]
    source = jnp.arange(N_BLK)[:, None, None]
    full = jnp.logical_or(owner == star, owner == source)
    return jnp.where(full, CAP, drawn).astype(jnp.int32)


def touch_ends(values, stream_key, low, high):
    shape = values.shape
    spot = [jax.random.randint(jax.random.fold_in(stream_key, axis), (), 0, shape[axis]) for axis in range(len(shape))]
    values = values.at[tuple(spot)].set(low)
    longest = shape.index(max(shape))
    spot[longest] = (spot[longest] + 1) % shape[longest]
    return values.at[tuple(spot)].set(high)


def steps_of(key, extent, split, least, top_value):
    loudness, own = 1.0, jax.random.fold_in(key, 6)
    for axis_at, shards_of in split:
        heights = jnp.exp(jax.random.uniform(jax.random.fold_in(own, axis_at), (shards_of,), jnp.float32, least / len(split), top_value / len(split)))
        loudness = loudness * jnp.repeat(heights, extent[axis_at] // shards_of).reshape([-1 if axis == axis_at else 1 for axis in range(len(extent))])
    return loudness


def gaussian(stream_key, extent, width, most, pieces=(), held_as=jnp.bfloat16):
    result = width * jax.random.normal(stream_key, extent, jnp.float32)
    if pieces:
        result = result * steps_of(stream_key, extent, pieces, -0.22, 0.18)
    return jnp.clip(result, -most, most).astype(held_as)


def setup_inputs(seed: int = 0, part: int = 0) -> dict:
    arg_keys = jax.random.split(jax.random.key(seed), 8)
    part_splits = jax.random.split(jax.random.fold_in(arg_keys[7], part), 8)
    aic = gaussian(part_splits[0], (ROWS, PANELS), PANELS ** -0.5, 0.03125, ((0, 4), (1, 4)), jnp.float32)
    downwash = gaussian(part_splits[1], (N_COL, PCOL, 2 * MODES), 1.0, 6.0, ((0, 4), (1, 4)), jnp.float32)
    node_modes = gaussian(arg_keys[2], (6, NODES, MODES), (6 * NODES) ** -0.5, 0.4375, ((1, 4),), jnp.float32)
    src_rows = touch_ends(jax.random.randint(arg_keys[3], (N_BLK, N_COL, N_BLK, CAP), 0, ROW_SUB), jax.random.fold_in(arg_keys[3], 1), 0, ROW_SUB - 1).astype(jnp.int32)
    dst_nodes = touch_ends(jax.random.randint(arg_keys[4], (N_BLK, N_COL, N_BLK, CAP), 0, NODE_DEV), jax.random.fold_in(arg_keys[4], 1), 0, NODE_DEV - 1).astype(jnp.int32)
    counts = draw_counts(jax.random.fold_in(arg_keys[7], 71), part)
    spline_weights = gaussian(arg_keys[6], (N_BLK, N_COL, 6, N_BLK, CAP), 0.1, 0.6, ((0, 4), (1, 4)), jnp.float32)
    return {"aic": aic, "downwash": downwash, "node_modes": node_modes, "src_rows": src_rows, "dst_nodes": dst_nodes, "counts": counts, "spline_weights": spline_weights}


def reference(aic, downwash, node_modes, src_rows, dst_nodes, counts, spline_weights):
    flat = downwash.reshape(PANELS, 2 * MODES)
    pressure = jnp.dot(aic, flat, precision=lax.Precision.HIGHEST, preferred_element_type=jnp.float32)
    sub_base = jnp.arange(N_COL, dtype=jnp.int32)[:, None, None] * ROW_SUB
    owner_base = jnp.arange(N_BLK, dtype=jnp.int32)[None, :, None] * NODE_DEV
    slot_index = jnp.arange(CAP, dtype=jnp.int32)[None, None, :]

    def add_block(loads, block_id):
        row_ids = (block_id * ROW_DEV + sub_base + src_rows[block_id]).astype(jnp.int32)
        node_ids = (owner_base + dst_nodes[block_id]).astype(jnp.int32)
        live = (slot_index < counts[block_id][:, :, None]).astype(jnp.float32)
        forces = pressure[row_ids]
        weights = jnp.transpose(spline_weights[block_id], (0, 2, 3, 1)) * live[..., None]
        weighted = weights[..., None] * forces[:, :, :, None, :]
        loads = loads.at[node_ids.reshape(-1)].add(weighted.reshape(-1, 6, 2 * MODES))
        return loads, None

    start = jnp.zeros((NODES, 6, 2 * MODES), jnp.float32)
    loads, unused = lax.scan(add_block, start, jnp.arange(N_BLK, dtype=jnp.int32))
    return jnp.einsum("dnm,ndk->mk", node_modes, loads, precision=lax.Precision.HIGHEST)
```

```python
import jax
import jax.numpy as jnp
from jax import lax
from jax.sharding import PartitionSpec as P


HIGHEST = lax.Precision.HIGHEST


def shifted(value, axis, steps):
    count = lax.axis_size(axis)
    pairs = [(source, (source + steps) % count) for source in range(count)]
    return lax.ppermute(value, axis, pairs)


def by_rotation(aic, downwash, node_modes, src_rows, dst_nodes, counts, spline_weights):
    cycle_size = lax.axis_size("blk")
    col_count = lax.axis_size("col")
    device = lax.axis_index("blk")
    own_block = downwash[0]
    panel_rows = own_block.shape[0]

    def product(shapes, source):
        columns = lax.dynamic_slice_in_dim(aic, source * panel_rows, panel_rows, 1)
        return jnp.dot(
            columns, shapes, precision=lax.Precision.HIGHEST, preferred_element_type=jnp.float32
        )

    halfway = cycle_size // 2

    def advance(offset, running):
        pressure, forward, behind = running
        forward = shifted(forward, "blk", 1)
        behind = shifted(behind, "blk", -1)
        pressure = pressure + product(forward, (device - offset) % cycle_size)
        pressure = pressure + product(behind, (device + offset) % cycle_size)
        return (pressure, forward, behind)

    pressure = product(own_block, device)
    pressure, forward, behind = lax.fori_loop(1, halfway, advance, (pressure, own_block, own_block))
    forward = shifted(forward, "blk", 1)
    pressure = pressure + product(forward, (device - halfway) % cycle_size)
    slots = src_rows.shape[-1]
    slot_index = jnp.arange(slots, dtype=jnp.int32)
    all_rows, all_nodes, all_counts = (
        lax.all_gather(src_rows, "col", axis=1, tiled=True),
        lax.all_gather(dst_nodes, "col", axis=1, tiled=True),
        lax.all_gather(counts, "col", axis=1, tiled=True),
    )
    weight_all = lax.all_gather(spline_weights, "col", axis=1, tiled=True)
    sub_rows = pressure.shape[0] // col_count
    offsets = jnp.arange(col_count, dtype=jnp.int32)[:, None, None] * sub_rows
    shifted_rows = all_rows[0] + offsets
    row_ids = jnp.transpose(shifted_rows, (1, 0, 2)).reshape(cycle_size, col_count * slots)
    node_ids = jnp.transpose(all_nodes[0], (1, 0, 2)).reshape(cycle_size, col_count * slots)
    live_sub = (slot_index[None, None, :] < all_counts[0][:, :, None]).astype(jnp.float32)
    live = jnp.transpose(live_sub, (1, 0, 2)).reshape(cycle_size, col_count * slots)
    weight_rows = jnp.transpose(weight_all[0], (1, 2, 0, 3)).reshape(
        6, cycle_size, col_count * slots
    )
    node_count = node_modes.shape[1]
    forces = pressure[row_ids.T]
    picks = (node_ids[None, :, :] == jnp.arange(node_count, dtype=jnp.int32)[:, None, None]).astype(
        jnp.float32
    )
    spread = weight_rows[:, None, :, :] * live[None, None, :, :] * picks[None, :, :, :]
    spread = spread.reshape(6 * node_count, cycle_size, row_ids.shape[1])
    arrived_forces, arrived_spread = (
        lax.all_to_all(forces, "blk", split_axis=1, concat_axis=1, tiled=True),
        lax.all_to_all(spread, "blk", split_axis=1, concat_axis=1, tiled=True),
    )
    loads = jnp.einsum(
        "jsc,csk->jk", arrived_spread, arrived_forces, precision=lax.Precision.HIGHEST
    )
    flat_modes = node_modes.reshape(6 * node_count, node_modes.shape[2])
    modal = jnp.einsum("jm,jk->mk", flat_modes, loads, precision=lax.Precision.HIGHEST)
    return lax.psum(modal, ("blk", "col"))


def by_collectives(aic, downwash, node_modes, src_rows, dst_nodes, counts, spline_weights):
    blocks = lax.axis_size("blk")
    col_count = lax.axis_size("col")
    dofs, node_count, modes = node_modes.shape
    slots = src_rows.shape[-1]
    rows = aic.shape[0]
    sub_rows = rows // col_count
    mine = lax.all_to_all(aic, "blk", split_axis=1, concat_axis=0, tiled=True)
    live = jnp.arange(slots, dtype=jnp.int32) < counts[0, 0][:, None]
    row_pick = src_rows[0, 0][..., None] == jnp.arange(sub_rows, dtype=jnp.int32)
    node_pick = dst_nodes[0, 0][..., None] == jnp.arange(node_count, dtype=jnp.int32)
    row_pick = jnp.where(live[..., None], row_pick.astype(jnp.float32), 0.0)
    weighted = spline_weights[0, 0][..., None] * node_pick.astype(jnp.float32)
    spline = jnp.einsum("osr,dosn->rdon", row_pick, weighted, precision=HIGHEST)
    spline = lax.all_gather(spline, ("blk", "col"), axis=0, tiled=True)
    every_mode = lax.all_gather(node_modes, "blk", axis=1, tiled=True)
    force = jnp.dot(
        spline.reshape(blocks * rows, dofs * blocks * node_count),
        every_mode.reshape(dofs * blocks * node_count, modes),
        precision=HIGHEST,
    )
    pressure = jnp.dot(mine, downwash[0], precision=HIGHEST, preferred_element_type=jnp.float32)
    part = lax.dot_general(force, pressure, (((0,), (0,)), ((), ())), precision=HIGHEST)
    return lax.psum(part, ("blk", "col"))


def solution(mesh):
    placed = (
        P(("groups", "blk"), "col"),
        P(("groups", "col"), "blk", None),
        P(None, "blk", None),
        P("blk", "col", None, None),
        P("blk", "col", None, None),
        P("blk", "col", None),
        P("blk", "col", None, None, None),
    )

    def shards(*operands):
        aic, node_modes = operands[0], operands[2]
        force_rows = lax.axis_size("blk") * aic.shape[0]
        if force_rows <= 2 * node_modes.shape[2]:
            return by_collectives(*operands)
        return by_rotation(*operands)

    return jax.shard_map(
        shards, mesh=mesh, in_specs=placed, out_specs=P("groups", None), check_vma=False
    )
```

```python
import functools

import jax
import jax.numpy as jnp
from jax import lax
from jax.experimental import pallas as pl
from jax.experimental.pallas import tpu as pltpu
from jax.sharding import PartitionSpec as P


HIGHEST = lax.Precision.HIGHEST


def shifted(value, axis, steps):
    count = lax.axis_size(axis)
    pairs = [(source, (source + steps) % count) for source in range(count)]
    return lax.ppermute(value, axis, pairs)


def by_rotation(aic, downwash, node_modes, src_rows, dst_nodes, counts, spline_weights):
    cycle_size = lax.axis_size("blk")
    col_count = lax.axis_size("col")
    device = lax.axis_index("blk")
    own_block = downwash[0]
    panel_rows = own_block.shape[0]

    def product(shapes, source):
        columns = lax.dynamic_slice_in_dim(aic, source * panel_rows, panel_rows, 1)
        return jnp.dot(
            columns, shapes, precision=lax.Precision.HIGHEST, preferred_element_type=jnp.float32
        )

    halfway = cycle_size // 2

    def advance(offset, running):
        pressure, forward, behind = running
        forward = shifted(forward, "blk", 1)
        behind = shifted(behind, "blk", -1)
        pressure = pressure + product(forward, (device - offset) % cycle_size)
        pressure = pressure + product(behind, (device + offset) % cycle_size)
        return (pressure, forward, behind)

    pressure = product(own_block, device)
    pressure, forward, behind = lax.fori_loop(1, halfway, advance, (pressure, own_block, own_block))
    forward = shifted(forward, "blk", 1)
    pressure = pressure + product(forward, (device - halfway) % cycle_size)
    slots = src_rows.shape[-1]
    slot_index = jnp.arange(slots, dtype=jnp.int32)
    all_rows, all_nodes, all_counts = (
        lax.all_gather(src_rows, "col", axis=1, tiled=True),
        lax.all_gather(dst_nodes, "col", axis=1, tiled=True),
        lax.all_gather(counts, "col", axis=1, tiled=True),
    )
    weight_all = lax.all_gather(spline_weights, "col", axis=1, tiled=True)
    sub_rows = pressure.shape[0] // col_count
    offsets = jnp.arange(col_count, dtype=jnp.int32)[:, None, None] * sub_rows
    shifted_rows = all_rows[0] + offsets
    row_ids = jnp.transpose(shifted_rows, (1, 0, 2)).reshape(cycle_size, col_count * slots)
    node_ids = jnp.transpose(all_nodes[0], (1, 0, 2)).reshape(cycle_size, col_count * slots)
    live_sub = (slot_index[None, None, :] < all_counts[0][:, :, None]).astype(jnp.float32)
    live = jnp.transpose(live_sub, (1, 0, 2)).reshape(cycle_size, col_count * slots)
    weight_rows = jnp.transpose(weight_all[0], (1, 2, 0, 3)).reshape(
        6, cycle_size, col_count * slots
    )
    node_count = node_modes.shape[1]
    forces = pressure[row_ids.T]
    picks = (node_ids[None, :, :] == jnp.arange(node_count, dtype=jnp.int32)[:, None, None]).astype(
        jnp.float32
    )
    spread = weight_rows[:, None, :, :] * live[None, None, :, :] * picks[None, :, :, :]
    spread = spread.reshape(6 * node_count, cycle_size, row_ids.shape[1])
    arrived_forces, arrived_spread = (
        lax.all_to_all(forces, "blk", split_axis=1, concat_axis=1, tiled=True),
        lax.all_to_all(spread, "blk", split_axis=1, concat_axis=1, tiled=True),
    )
    loads = jnp.einsum(
        "jsc,csk->jk", arrived_spread, arrived_forces, precision=lax.Precision.HIGHEST
    )
    flat_modes = node_modes.reshape(6 * node_count, node_modes.shape[2])
    modal = jnp.einsum("jm,jk->mk", flat_modes, loads, precision=lax.Precision.HIGHEST)
    return lax.psum(modal, ("blk", "col"))


def split(value):
    high = value.astype(jnp.bfloat16)
    low = (value - high.astype(jnp.float32)).astype(jnp.bfloat16)
    return high, low


def exchange_kernel(
    blocks,
    cols,
    aic,
    panels,
    node_modes,
    rows_list,
    nodes_list,
    counts,
    weights,
    out,
    influence,
    shapes,
    shapes_high,
    shapes_low,
    partial,
    plane_in,
    line_in,
    pressure,
    spline,
    mode_rows,
    force,
    local_sem,
    aic_send,
    aic_recv,
    plane_send,
    plane_recv,
    line_send,
    line_recv,
    final_send,
    final_recv,
    spline_send,
    spline_recv,
    mode_send,
    mode_recv,
):
    b = lax.axis_index("blk")
    c = lax.axis_index("col")
    chunks, _, sub, depth = influence.shape
    dofs, _, node_count, modes = mode_rows.shape
    owners, slots = rows_list.shape[2:]
    width = panels.shape[2]
    senders = min(cols, dofs)
    while dofs % senders:
        senders -= 1
    share = dofs // senders
    pieces = local_sem.shape[0] - chunks - 1
    piece = depth // pieces

    def on_line(k):
        return lax.rem(b + k, blocks)

    def on_plane(k):
        return lax.rem(c + k, cols)

    def to_line(k, source, target, send, recv):
        return pltpu.make_async_remote_copy(
            src_ref=source,
            dst_ref=target,
            send_sem=send,
            recv_sem=recv,
            device_id={"blk": on_line(k)},
            device_id_type=pl.DeviceIdType.MESH,
        )

    def to_plane(k, source, target, send, recv):
        return pltpu.make_async_remote_copy(
            src_ref=source,
            dst_ref=target,
            send_sem=send,
            recv_sem=recv,
            device_id={"col": on_plane(k)},
            device_id_type=pl.DeviceIdType.MESH,
        )

    shape_copies = []
    for p in range(pieces):
        span = pl.ds(p * piece, piece)
        shape_copies.append(
            pltpu.make_async_copy(panels.at[0, span], shapes.at[span], local_sem.at[p])
        )
        shape_copies[-1].start()
    own_copies = []
    for q in range(chunks):
        own_copies.append(
            pltpu.make_async_copy(
                aic.at[pl.ds(q * sub, sub), pl.ds(pl.multiple_of(b * depth, depth), depth)],
                influence.at[q, b],
                local_sem.at[pieces + q],
            )
        )
        own_copies[-1].start()
    dof_span = pl.ds(lax.rem(c, senders) * share, share)
    own_modes = pltpu.make_async_copy(
        node_modes.at[dof_span], mode_rows.at[dof_span, b], local_sem.at[pieces + chunks]
    )

    barrier = pltpu.get_barrier_semaphore()
    for k in range(1, blocks):
        pl.semaphore_signal(
            barrier, inc=1, device_id={"blk": on_line(k)}, device_id_type=pl.DeviceIdType.MESH
        )
    for k in range(1, cols):
        pl.semaphore_signal(
            barrier, inc=1, device_id={"col": on_plane(k)}, device_id_type=pl.DeviceIdType.MESH
        )
    pl.semaphore_wait(barrier, blocks + cols - 2)

    aic_out = {}

    def send_rows(q):
        for k in range(1, blocks):
            peer = on_line(k)
            copy = to_line(
                k,
                aic.at[pl.ds(q * sub, sub), pl.ds(pl.multiple_of(peer * depth, depth), depth)],
                influence.at[q, b],
                aic_send.at[q, k - 1],
                aic_recv.at[q, k - 1],
            )
            copy.start()
            aic_out[q, k] = copy

    ahead = min(2, chunks)
    for q in range(ahead):
        send_rows(q)
        if q == 0:
            mode_out = [
                to_line(
                    k,
                    node_modes.at[dof_span],
                    mode_rows.at[dof_span, b],
                    mode_send.at[k - 1],
                    mode_recv.at[k - 1],
                )
                for k in range(1, blocks)
            ]

            @pl.when(c < senders)
            def _():
                own_modes.start()
                for copy in mode_out:
                    copy.start()

            length = dofs * owners * node_count
            row_at = lax.broadcasted_iota(jnp.int32, (sub, length), 0)
            column_at = lax.broadcasted_iota(jnp.int32, (sub, length), 1)
            total = jnp.zeros((sub, length), jnp.float32)
            for o in range(owners):
                for s in range(slots):
                    live = s < counts[0, 0, o]
                    row = jnp.where(live, rows_list[0, 0, o, s], -1)
                    node = nodes_list[0, 0, o, s] + o * node_count
                    spread = jnp.zeros((sub, length), jnp.float32)
                    for d in range(dofs):
                        spread = jnp.where(
                            column_at == node + d * owners * node_count,
                            weights[0, 0, d, o, s],
                            spread,
                        )
                    total = total + jnp.where(row_at == row, spread, 0.0)
            spline[c, b] = total
            spline_out = []
            for k in range(1, blocks):
                copy = to_line(
                    k,
                    spline.at[c, b],
                    spline.at[c, b],
                    spline_send.at[k - 1],
                    spline_recv.at[k - 1],
                )
                copy.start()
                spline_out.append(copy)

    for p in range(pieces):
        shape_copies[p].wait()
        span = pl.ds(p * piece, piece)
        high, low = split(shapes[span])
        shapes_high[span] = high
        shapes_low[span] = low

    for copy in spline_out:
        copy.wait()
    for k in range(1, cols):
        copy = to_plane(
            k,
            spline.at[c],
            spline.at[c],
            spline_send.at[blocks - 2 + k],
            spline_recv.at[blocks - 2 + k],
        )
        copy.start()
        spline_out.append(copy)
    mode_plane = [
        to_plane(
            k,
            mode_rows.at[dof_span],
            mode_rows.at[dof_span],
            mode_send.at[blocks - 2 + k],
            mode_recv.at[blocks - 2 + k],
        )
        for k in range(1, cols)
    ]

    @pl.when(c < senders)
    def _():
        own_modes.wait()
        for copy in mode_out:
            copy.wait()
        for copy in mode_plane:
            copy.start()

    plane_out, line_out, final_out = {}, {}, {}

    def await_rows(q):
        own_copies[q].wait()
        for k in range(1, blocks):
            aic_out[q, k].wait_recv()

    def multiply(q):
        high, low = split(influence[q].reshape(blocks * sub, depth))
        product = jnp.dot(
            jnp.concatenate([high, low], axis=0),
            shapes_high[...],
            preferred_element_type=jnp.float32,
        )
        rest = jnp.dot(high, shapes_low[...], preferred_element_type=jnp.float32)
        lines = blocks * sub
        product = product[:lines] + (product[lines:] + rest)
        partial[q] = product.reshape(blocks, sub, width)
        for k in range(1, cols):
            copy = to_plane(
                k,
                partial.at[q, on_plane(k)],
                plane_in.at[q, k - 1],
                plane_send.at[q, k - 1],
                plane_recv.at[q, k - 1],
            )
            copy.start()
            plane_out[q, k] = copy

    def over_plane(q):
        total = partial[q, c]
        for k in range(1, cols):
            plane_out[q, k].wait_recv()
            total = total + plane_in[q, k - 1]
        line_in[q, b] = total
        for k in range(1, blocks):
            copy = to_line(
                k,
                line_in.at[q, b],
                line_in.at[q, b],
                line_send.at[q, k - 1],
                line_recv.at[q, k - 1],
            )
            copy.start()
            line_out[q, k] = copy

    def over_line(q):
        for k in range(1, blocks):
            line_out[q, k].wait_recv()
        total = line_in[q, 0]
        for source in range(1, blocks):
            total = total + line_in[q, source]
        pressure[q, c] = total
        for k in range(1, cols):
            copy = to_plane(
                k,
                pressure.at[q, c],
                pressure.at[q, c],
                final_send.at[q, k - 1],
                final_recv.at[q, k - 1],
            )
            copy.start()
            final_out[q, k] = copy

    def make_force():
        for k in range(1, cols):
            spline_out[blocks - 2 + k].wait_recv()

            @pl.when(lax.rem(c + cols - k, cols) < senders)
            def _():
                mode_plane[k - 1].wait_recv()

        length = dofs * owners * node_count
        force[...] = jnp.dot(
            spline[...].reshape(cols * blocks * sub, length),
            mode_rows[...].reshape(length, modes),
            precision=HIGHEST,
            preferred_element_type=jnp.float32,
        )

    for q in range(chunks):
        await_rows(q)
        if q >= 1:
            over_plane(q - 1)
        if q + ahead < chunks:
            send_rows(q + ahead)
        multiply(q)
        if q == 0:
            make_force()
        if q >= 2:
            over_line(q - 2)
    if chunks >= 2:
        over_line(chunks - 2)
    over_plane(chunks - 1)
    over_line(chunks - 1)
    for q in range(chunks):
        for k in range(1, cols):
            final_out[q, k].wait_recv()
    out[...] = lax.dot_general(
        force[...],
        pressure[...].reshape(chunks * blocks * sub, width),
        (((0,), (0,)), ((), ())),
        precision=HIGHEST,
        preferred_element_type=jnp.float32,
    )

    for copy in spline_out[blocks - 1 :]:
        copy.wait_send()
    for group in (aic_out, plane_out, line_out, final_out):
        for copy in group.values():
            copy.wait_send()

    @pl.when(c < senders)
    def _():
        for copy in mode_plane:
            copy.wait_send()


def by_kernel(aic, downwash, node_modes, src_rows, dst_nodes, counts, spline_weights):
    blocks = lax.axis_size("blk")
    cols = lax.axis_size("col")
    rows = aic.shape[0]
    sub = rows // cols
    depth, width = downwash.shape[1:]
    dofs, node_count, modes = node_modes.shape
    length = dofs * blocks * node_count
    pieces = 4
    dma = pltpu.SemaphoreType.DMA
    anywhere = pl.BlockSpec(memory_space=pl.ANY)
    scalars = pl.BlockSpec(memory_space=pltpu.SMEM)
    return pl.pallas_call(
        functools.partial(exchange_kernel, blocks, cols),
        name="gaf_exchange",
        out_shape=jax.ShapeDtypeStruct((modes, width), jnp.float32),
        in_specs=[anywhere, anywhere, anywhere, scalars, scalars, scalars, scalars],
        out_specs=pl.BlockSpec(memory_space=pltpu.VMEM),
        scratch_shapes=[
            pltpu.VMEM((cols, blocks, sub, depth), jnp.float32),
            pltpu.VMEM((depth, width), jnp.float32),
            pltpu.VMEM((depth, width), jnp.bfloat16),
            pltpu.VMEM((depth, width), jnp.bfloat16),
            pltpu.VMEM((cols, blocks, sub, width), jnp.float32),
            pltpu.VMEM((cols, cols - 1, sub, width), jnp.float32),
            pltpu.VMEM((cols, blocks, sub, width), jnp.float32),
            pltpu.VMEM((cols, blocks, sub, width), jnp.float32),
            pltpu.VMEM((cols, blocks, sub, length), jnp.float32),
            pltpu.VMEM((dofs, blocks, node_count, modes), jnp.float32),
            pltpu.VMEM((cols * blocks * sub, modes), jnp.float32),
            dma((pieces + cols + 1,)),
            dma((cols, blocks - 1)),
            dma((cols, blocks - 1)),
            dma((cols, cols - 1)),
            dma((cols, cols - 1)),
            dma((cols, blocks - 1)),
            dma((cols, blocks - 1)),
            dma((cols, cols - 1)),
            dma((cols, cols - 1)),
            dma((blocks + cols - 2,)),
            dma((blocks + cols - 2,)),
            dma((blocks + cols - 2,)),
            dma((blocks + cols - 2,)),
        ],
        compiler_params=pltpu.CompilerParams(
            collective_id=0, has_side_effects=True, vmem_limit_bytes=60 * 1024 * 1024
        ),
    )(aic, downwash, node_modes, src_rows, dst_nodes, counts, spline_weights)


def solution(mesh):
    placed = (
        P(("groups", "blk"), "col"),
        P(("groups", "col"), "blk", None),
        P(None, "blk", None),
        P("blk", "col", None, None),
        P("blk", "col", None, None),
        P("blk", "col", None),
        P("blk", "col", None, None, None),
    )

    def shards(*operands):
        aic, downwash, node_modes = operands[:3]
        blocks, cols = lax.axis_size("blk"), lax.axis_size("col")
        small = blocks * aic.shape[0] <= 2 * node_modes.shape[2]
        even = blocks == cols and aic.shape[0] % (8 * cols) == 0 and downwash.shape[1] % 512 == 0
        if small and even:
            return by_kernel(*operands)
        return by_rotation(*operands)

    return jax.shard_map(
        shards, mesh=mesh, in_specs=placed, out_specs=P("groups", None), check_vma=False
    )
```

```python
import functools

import jax
import jax.numpy as jnp
from jax import lax
from jax.experimental import pallas as pl
from jax.experimental.pallas import tpu as pltpu
from jax.sharding import PartitionSpec as P


HIGHEST = lax.Precision.HIGHEST


def shifted(value, axis, steps):
    count = lax.axis_size(axis)
    pairs = [(source, (source + steps) % count) for source in range(count)]
    return lax.ppermute(value, axis, pairs)


def by_rotation(aic, downwash, node_modes, src_rows, dst_nodes, counts, spline_weights):
    cycle_size = lax.axis_size("blk")
    col_count = lax.axis_size("col")
    device = lax.axis_index("blk")
    own_block = downwash[0]
    panel_rows = own_block.shape[0]

    def product(shapes, source):
        columns = lax.dynamic_slice_in_dim(aic, source * panel_rows, panel_rows, 1)
        return jnp.dot(
            columns, shapes, precision=lax.Precision.HIGHEST, preferred_element_type=jnp.float32
        )

    halfway = cycle_size // 2

    def advance(offset, running):
        pressure, forward, behind = running
        forward = shifted(forward, "blk", 1)
        behind = shifted(behind, "blk", -1)
        pressure = pressure + product(forward, (device - offset) % cycle_size)
        pressure = pressure + product(behind, (device + offset) % cycle_size)
        return (pressure, forward, behind)

    pressure = product(own_block, device)
    pressure, forward, behind = lax.fori_loop(1, halfway, advance, (pressure, own_block, own_block))
    forward = shifted(forward, "blk", 1)
    pressure = pressure + product(forward, (device - halfway) % cycle_size)
    slots = src_rows.shape[-1]
    slot_index = jnp.arange(slots, dtype=jnp.int32)
    all_rows, all_nodes, all_counts = (
        lax.all_gather(src_rows, "col", axis=1, tiled=True),
        lax.all_gather(dst_nodes, "col", axis=1, tiled=True),
        lax.all_gather(counts, "col", axis=1, tiled=True),
    )
    weight_all = lax.all_gather(spline_weights, "col", axis=1, tiled=True)
    sub_rows = pressure.shape[0] // col_count
    offsets = jnp.arange(col_count, dtype=jnp.int32)[:, None, None] * sub_rows
    shifted_rows = all_rows[0] + offsets
    row_ids = jnp.transpose(shifted_rows, (1, 0, 2)).reshape(cycle_size, col_count * slots)
    node_ids = jnp.transpose(all_nodes[0], (1, 0, 2)).reshape(cycle_size, col_count * slots)
    live_sub = (slot_index[None, None, :] < all_counts[0][:, :, None]).astype(jnp.float32)
    live = jnp.transpose(live_sub, (1, 0, 2)).reshape(cycle_size, col_count * slots)
    weight_rows = jnp.transpose(weight_all[0], (1, 2, 0, 3)).reshape(
        6, cycle_size, col_count * slots
    )
    node_count = node_modes.shape[1]
    forces = pressure[row_ids.T]
    picks = (node_ids[None, :, :] == jnp.arange(node_count, dtype=jnp.int32)[:, None, None]).astype(
        jnp.float32
    )
    spread = weight_rows[:, None, :, :] * live[None, None, :, :] * picks[None, :, :, :]
    spread = spread.reshape(6 * node_count, cycle_size, row_ids.shape[1])
    arrived_forces, arrived_spread = (
        lax.all_to_all(forces, "blk", split_axis=1, concat_axis=1, tiled=True),
        lax.all_to_all(spread, "blk", split_axis=1, concat_axis=1, tiled=True),
    )
    loads = jnp.einsum(
        "jsc,csk->jk", arrived_spread, arrived_forces, precision=lax.Precision.HIGHEST
    )
    flat_modes = node_modes.reshape(6 * node_count, node_modes.shape[2])
    modal = jnp.einsum("jm,jk->mk", flat_modes, loads, precision=lax.Precision.HIGHEST)
    return lax.psum(modal, ("blk", "col"))


def split(value):
    high = value.astype(jnp.bfloat16)
    low = (value - high.astype(jnp.float32)).astype(jnp.bfloat16)
    return high, low


def exchange_kernel(
    blocks,
    cols,
    aic,
    panels,
    node_modes,
    rows_hbm,
    nodes_hbm,
    counts_hbm,
    weights_hbm,
    out,
    influence,
    shapes,
    shapes_high,
    shapes_low,
    partial,
    plane_in,
    line_in,
    pressure,
    spline,
    mode_rows,
    force,
    rows_list,
    nodes_list,
    counts,
    weights,
    list_sem,
    local_sem,
    aic_send,
    aic_recv,
    plane_send,
    plane_recv,
    line_send,
    line_recv,
    final_send,
    final_recv,
    spline_send,
    spline_recv,
    mode_send,
    mode_recv,
):
    b = lax.axis_index("blk")
    c = lax.axis_index("col")
    chunks, _, sub, depth = influence.shape
    dofs, _, node_count, modes = mode_rows.shape
    owners, slots = rows_list.shape[2:]
    width = panels.shape[2]
    senders = min(cols, dofs)
    while dofs % senders:
        senders -= 1
    share = dofs // senders
    pieces = local_sem.shape[0] - chunks - 1
    piece = depth // pieces

    def on_line(k):
        return lax.rem(b + k, blocks)

    def on_plane(k):
        return lax.rem(c + k, cols)

    def to_line(k, source, target, send, recv):
        return pltpu.make_async_remote_copy(
            src_ref=source,
            dst_ref=target,
            send_sem=send,
            recv_sem=recv,
            device_id={"blk": on_line(k)},
            device_id_type=pl.DeviceIdType.MESH,
        )

    def to_plane(k, source, target, send, recv):
        return pltpu.make_async_remote_copy(
            src_ref=source,
            dst_ref=target,
            send_sem=send,
            recv_sem=recv,
            device_id={"col": on_plane(k)},
            device_id_type=pl.DeviceIdType.MESH,
        )

    list_copies = []
    lists = ((rows_hbm, rows_list), (nodes_hbm, nodes_list), (counts_hbm, counts), (weights_hbm, weights))
    for i, (source, target) in enumerate(lists):
        list_copies.append(pltpu.make_async_copy(source, target, list_sem.at[i]))
        list_copies[-1].start()
    shape_copies = []
    for p in range(pieces):
        span = pl.ds(p * piece, piece)
        shape_copies.append(
            pltpu.make_async_copy(panels.at[0, span], shapes.at[span], local_sem.at[p])
        )
        shape_copies[-1].start()
    own_copies = []
    for q in range(chunks):
        own_copies.append(
            pltpu.make_async_copy(
                aic.at[pl.ds(q * sub, sub), pl.ds(pl.multiple_of(b * depth, depth), depth)],
                influence.at[q, b],
                local_sem.at[pieces + q],
            )
        )
        own_copies[-1].start()
    dof_span = pl.ds(lax.rem(c, senders) * share, share)
    own_modes = pltpu.make_async_copy(
        node_modes.at[dof_span], mode_rows.at[dof_span, b], local_sem.at[pieces + chunks]
    )

    barrier = pltpu.get_barrier_semaphore()
    for k in range(1, blocks):
        pl.semaphore_signal(
            barrier, inc=1, device_id={"blk": on_line(k)}, device_id_type=pl.DeviceIdType.MESH
        )
    for k in range(1, cols):
        pl.semaphore_signal(
            barrier, inc=1, device_id={"col": on_plane(k)}, device_id_type=pl.DeviceIdType.MESH
        )
    pl.semaphore_wait(barrier, blocks + cols - 2)

    aic_out = {}

    def send_rows(q):
        for k in range(1, blocks):
            peer = on_line(k)
            copy = to_line(
                k,
                aic.at[pl.ds(q * sub, sub), pl.ds(pl.multiple_of(peer * depth, depth), depth)],
                influence.at[q, b],
                aic_send.at[q, k - 1],
                aic_recv.at[q, k - 1],
            )
            copy.start()
            aic_out[q, k] = copy

    ahead = min(2, chunks)
    for q in range(ahead):
        send_rows(q)
        if q == 0:
            mode_out = [
                to_line(
                    k,
                    node_modes.at[dof_span],
                    mode_rows.at[dof_span, b],
                    mode_send.at[k - 1],
                    mode_recv.at[k - 1],
                )
                for k in range(1, blocks)
            ]

            @pl.when(c < senders)
            def _():
                own_modes.start()
                for copy in mode_out:
                    copy.start()

            length = dofs * owners * node_count
            row_at = lax.broadcasted_iota(jnp.int32, (sub, length), 0)
            column_at = lax.broadcasted_iota(jnp.int32, (sub, length), 1)
            total = jnp.zeros((sub, length), jnp.float32)
            for copy in list_copies:
                copy.wait()
            for o in range(owners):
                for s in range(slots):
                    live = s < counts[0, 0, o]
                    row = jnp.where(live, rows_list[0, 0, o, s], -1)
                    node = nodes_list[0, 0, o, s] + o * node_count
                    spread = jnp.zeros((sub, length), jnp.float32)
                    for d in range(dofs):
                        spread = jnp.where(
                            column_at == node + d * owners * node_count,
                            weights[0, 0, d, o, s],
                            spread,
                        )
                    total = total + jnp.where(row_at == row, spread, 0.0)
            spline[c, b] = total
            spline_out = []
            for k in range(1, blocks):
                copy = to_line(
                    k,
                    spline.at[c, b],
                    spline.at[c, b],
                    spline_send.at[k - 1],
                    spline_recv.at[k - 1],
                )
                copy.start()
                spline_out.append(copy)

    for p in range(pieces):
        shape_copies[p].wait()
        span = pl.ds(p * piece, piece)
        high, low = split(shapes[span])
        shapes_high[span] = high
        shapes_low[span] = low

    for copy in spline_out:
        copy.wait()
    for k in range(1, cols):
        copy = to_plane(
            k,
            spline.at[c],
            spline.at[c],
            spline_send.at[blocks - 2 + k],
            spline_recv.at[blocks - 2 + k],
        )
        copy.start()
        spline_out.append(copy)
    mode_plane = [
        to_plane(
            k,
            mode_rows.at[dof_span],
            mode_rows.at[dof_span],
            mode_send.at[blocks - 2 + k],
            mode_recv.at[blocks - 2 + k],
        )
        for k in range(1, cols)
    ]

    @pl.when(c < senders)
    def _():
        own_modes.wait()
        for copy in mode_out:
            copy.wait()
        for copy in mode_plane:
            copy.start()

    plane_out, line_out, final_out = {}, {}, {}

    def await_rows(q):
        own_copies[q].wait()
        for k in range(1, blocks):
            aic_out[q, k].wait_recv()

    def multiply(q):
        high, low = split(influence[q].reshape(blocks * sub, depth))
        product = jnp.dot(
            jnp.concatenate([high, low], axis=0),
            shapes_high[...],
            preferred_element_type=jnp.float32,
        )
        rest = jnp.dot(high, shapes_low[...], preferred_element_type=jnp.float32)
        lines = blocks * sub
        product = product[:lines] + (product[lines:] + rest)
        partial[q] = product.reshape(blocks, sub, width)
        for k in range(1, cols):
            copy = to_plane(
                k,
                partial.at[q, on_plane(k)],
                plane_in.at[q, k - 1],
                plane_send.at[q, k - 1],
                plane_recv.at[q, k - 1],
            )
            copy.start()
            plane_out[q, k] = copy

    def over_plane(q):
        total = partial[q, c]
        for k in range(1, cols):
            plane_out[q, k].wait_recv()
            total = total + plane_in[q, k - 1]
        line_in[q, b] = total
        for k in range(1, blocks):
            copy = to_line(
                k,
                line_in.at[q, b],
                line_in.at[q, b],
                line_send.at[q, k - 1],
                line_recv.at[q, k - 1],
            )
            copy.start()
            line_out[q, k] = copy

    def over_line(q):
        for k in range(1, blocks):
            line_out[q, k].wait_recv()
        total = line_in[q, 0]
        for source in range(1, blocks):
            total = total + line_in[q, source]
        pressure[q, c] = total
        for k in range(1, cols):
            copy = to_plane(
                k,
                pressure.at[q, c],
                pressure.at[q, c],
                final_send.at[q, k - 1],
                final_recv.at[q, k - 1],
            )
            copy.start()
            final_out[q, k] = copy

    def make_force():
        for k in range(1, cols):
            spline_out[blocks - 2 + k].wait_recv()

            @pl.when(lax.rem(c + cols - k, cols) < senders)
            def _():
                mode_plane[k - 1].wait_recv()

        length = dofs * owners * node_count
        force[...] = jnp.dot(
            spline[...].reshape(cols * blocks * sub, length),
            mode_rows[...].reshape(length, modes),
            precision=HIGHEST,
            preferred_element_type=jnp.float32,
        )

    def modal(start, stop):
        force_rows = force[pl.ds(start * blocks * sub, (stop - start) * blocks * sub)]
        return lax.dot_general(
            force_rows,
            pressure[start:stop].reshape((stop - start) * blocks * sub, width),
            (((0,), (0,)), ((), ())),
            precision=HIGHEST,
            preferred_element_type=jnp.float32,
        )

    def await_pressure(q):
        for k in range(1, cols):
            final_out[q, k].wait_recv()

    for q in range(chunks):
        await_rows(q)
        multiply(q)
        over_plane(q)
        if q + ahead < chunks:
            send_rows(q + ahead)
        if q == 0:
            make_force()
        else:
            over_line(q - 1)
    last = chunks - 1
    over_line(last)
    if last:
        for q in range(last):
            await_pressure(q)
        out[...] = modal(0, last)
        await_pressure(last)
        out[...] += modal(last, chunks)
    else:
        await_pressure(last)
        out[...] = modal(last, chunks)

    for copy in spline_out[blocks - 1 :]:
        copy.wait_send()
    for group in (aic_out, plane_out, line_out, final_out):
        for copy in group.values():
            copy.wait_send()

    @pl.when(c < senders)
    def _():
        for copy in mode_plane:
            copy.wait_send()


def by_kernel(aic, downwash, node_modes, src_rows, dst_nodes, counts, spline_weights):
    blocks = lax.axis_size("blk")
    cols = lax.axis_size("col")
    rows = aic.shape[0]
    sub = rows // cols
    depth, width = downwash.shape[1:]
    dofs, node_count, modes = node_modes.shape
    length = dofs * blocks * node_count
    pieces = 4
    dma = pltpu.SemaphoreType.DMA
    anywhere = pl.BlockSpec(memory_space=pl.ANY)
    return pl.pallas_call(
        functools.partial(exchange_kernel, blocks, cols),
        name="gaf_exchange",
        out_shape=jax.ShapeDtypeStruct((modes, width), jnp.float32),
        in_specs=[anywhere] * 7,
        out_specs=pl.BlockSpec(memory_space=pltpu.VMEM),
        scratch_shapes=[
            pltpu.VMEM((cols, blocks, sub, depth), jnp.float32),
            pltpu.VMEM((depth, width), jnp.float32),
            pltpu.VMEM((depth, width), jnp.bfloat16),
            pltpu.VMEM((depth, width), jnp.bfloat16),
            pltpu.VMEM((cols, blocks, sub, width), jnp.float32),
            pltpu.VMEM((cols, cols - 1, sub, width), jnp.float32),
            pltpu.VMEM((cols, blocks, sub, width), jnp.float32),
            pltpu.VMEM((cols, blocks, sub, width), jnp.float32),
            pltpu.VMEM((cols, blocks, sub, length), jnp.float32),
            pltpu.VMEM((dofs, blocks, node_count, modes), jnp.float32),
            pltpu.VMEM((cols * blocks * sub, modes), jnp.float32),
            pltpu.SMEM(src_rows.shape, jnp.int32),
            pltpu.SMEM(dst_nodes.shape, jnp.int32),
            pltpu.SMEM(counts.shape, jnp.int32),
            pltpu.SMEM(spline_weights.shape, jnp.float32),
            dma((4,)),
            dma((pieces + cols + 1,)),
            dma((cols, blocks - 1)),
            dma((cols, blocks - 1)),
            dma((cols, cols - 1)),
            dma((cols, cols - 1)),
            dma((cols, blocks - 1)),
            dma((cols, blocks - 1)),
            dma((cols, cols - 1)),
            dma((cols, cols - 1)),
            dma((blocks + cols - 2,)),
            dma((blocks + cols - 2,)),
            dma((blocks + cols - 2,)),
            dma((blocks + cols - 2,)),
        ],
        compiler_params=pltpu.CompilerParams(
            collective_id=0, has_side_effects=True, vmem_limit_bytes=60 * 1024 * 1024
        ),
    )(aic, downwash, node_modes, src_rows, dst_nodes, counts, spline_weights)


def solution(mesh):
    placed = (
        P(("groups", "blk"), "col"),
        P(("groups", "col"), "blk", None),
        P(None, "blk", None),
        P("blk", "col", None, None),
        P("blk", "col", None, None),
        P("blk", "col", None),
        P("blk", "col", None, None, None),
    )

    def shards(*operands):
        aic, downwash, node_modes = operands[:3]
        blocks, cols = lax.axis_size("blk"), lax.axis_size("col")
        small = blocks * aic.shape[0] <= 2 * node_modes.shape[2]
        even = blocks == cols and aic.shape[0] % (8 * cols) == 0 and downwash.shape[1] % 512 == 0
        if small and even:
            return by_kernel(*operands)
        return by_rotation(*operands)

    return jax.shard_map(
        shards, mesh=mesh, in_specs=placed, out_specs=P("groups", None), check_vma=False
    )
```

```python
import functools

import jax
import jax.numpy as jnp
from jax import lax
from jax.experimental import pallas as pl
from jax.experimental.pallas import tpu as pltpu
from jax.sharding import PartitionSpec as P


HIGHEST = lax.Precision.HIGHEST


def shifted(value, axis, steps):
    count = lax.axis_size(axis)
    pairs = [(source, (source + steps) % count) for source in range(count)]
    return lax.ppermute(value, axis, pairs)


def by_rotation(aic, downwash, node_modes, src_rows, dst_nodes, counts, spline_weights):
    cycle_size = lax.axis_size("blk")
    col_count = lax.axis_size("col")
    device = lax.axis_index("blk")
    own_block = downwash[0]
    panel_rows = own_block.shape[0]

    def product(shapes, source):
        columns = lax.dynamic_slice_in_dim(aic, source * panel_rows, panel_rows, 1)
        return jnp.dot(
            columns, shapes, precision=lax.Precision.HIGHEST, preferred_element_type=jnp.float32
        )

    halfway = cycle_size // 2

    def advance(offset, running):
        pressure, forward, behind = running
        forward = shifted(forward, "blk", 1)
        behind = shifted(behind, "blk", -1)
        pressure = pressure + product(forward, (device - offset) % cycle_size)
        pressure = pressure + product(behind, (device + offset) % cycle_size)
        return (pressure, forward, behind)

    pressure = product(own_block, device)
    pressure, forward, behind = lax.fori_loop(1, halfway, advance, (pressure, own_block, own_block))
    forward = shifted(forward, "blk", 1)
    pressure = pressure + product(forward, (device - halfway) % cycle_size)
    slots = src_rows.shape[-1]
    slot_index = jnp.arange(slots, dtype=jnp.int32)
    all_rows, all_nodes, all_counts = (
        lax.all_gather(src_rows, "col", axis=1, tiled=True),
        lax.all_gather(dst_nodes, "col", axis=1, tiled=True),
        lax.all_gather(counts, "col", axis=1, tiled=True),
    )
    weight_all = lax.all_gather(spline_weights, "col", axis=1, tiled=True)
    sub_rows = pressure.shape[0] // col_count
    offsets = jnp.arange(col_count, dtype=jnp.int32)[:, None, None] * sub_rows
    shifted_rows = all_rows[0] + offsets
    row_ids = jnp.transpose(shifted_rows, (1, 0, 2)).reshape(cycle_size, col_count * slots)
    node_ids = jnp.transpose(all_nodes[0], (1, 0, 2)).reshape(cycle_size, col_count * slots)
    live_sub = (slot_index[None, None, :] < all_counts[0][:, :, None]).astype(jnp.float32)
    live = jnp.transpose(live_sub, (1, 0, 2)).reshape(cycle_size, col_count * slots)
    weight_rows = jnp.transpose(weight_all[0], (1, 2, 0, 3)).reshape(
        6, cycle_size, col_count * slots
    )
    node_count = node_modes.shape[1]
    forces = pressure[row_ids.T]
    picks = (node_ids[None, :, :] == jnp.arange(node_count, dtype=jnp.int32)[:, None, None]).astype(
        jnp.float32
    )
    spread = weight_rows[:, None, :, :] * live[None, None, :, :] * picks[None, :, :, :]
    spread = spread.reshape(6 * node_count, cycle_size, row_ids.shape[1])
    arrived_forces, arrived_spread = (
        lax.all_to_all(forces, "blk", split_axis=1, concat_axis=1, tiled=True),
        lax.all_to_all(spread, "blk", split_axis=1, concat_axis=1, tiled=True),
    )
    loads = jnp.einsum(
        "jsc,csk->jk", arrived_spread, arrived_forces, precision=lax.Precision.HIGHEST
    )
    flat_modes = node_modes.reshape(6 * node_count, node_modes.shape[2])
    modal = jnp.einsum("jm,jk->mk", flat_modes, loads, precision=lax.Precision.HIGHEST)
    return lax.psum(modal, ("blk", "col"))


def split(value):
    high = value.astype(jnp.bfloat16)
    low = (value - high.astype(jnp.float32)).astype(jnp.bfloat16)
    return high, low


def exchange_kernel(
    blocks,
    cols,
    aic,
    panels,
    node_modes,
    rows_hbm,
    nodes_hbm,
    counts_hbm,
    weights_hbm,
    out,
    influence,
    shapes,
    shapes_high,
    shapes_low,
    partial,
    plane_in,
    line_in,
    pressure,
    spline,
    mode_rows,
    force,
    rows_list,
    nodes_list,
    counts,
    weights,
    list_sem,
    local_sem,
    aic_send,
    aic_recv,
    plane_send,
    plane_recv,
    line_send,
    line_recv,
    final_send,
    final_recv,
    spline_send,
    spline_recv,
    mode_send,
    mode_recv,
):
    b = lax.axis_index("blk")
    c = lax.axis_index("col")
    chunks, _, sub, depth = influence.shape
    dofs, _, node_count, modes = mode_rows.shape
    owners, slots = rows_list.shape[2:]
    width = panels.shape[2]
    senders = min(cols, dofs)
    while dofs % senders:
        senders -= 1
    share = dofs // senders
    pieces = local_sem.shape[0] - chunks - 1
    piece = depth // pieces

    def on_line(k):
        return lax.rem(b + k, blocks)

    def on_plane(k):
        return lax.rem(c + k, cols)

    def to_line(k, source, target, send, recv):
        return pltpu.make_async_remote_copy(
            src_ref=source,
            dst_ref=target,
            send_sem=send,
            recv_sem=recv,
            device_id={"blk": on_line(k)},
            device_id_type=pl.DeviceIdType.MESH,
        )

    def to_plane(k, source, target, send, recv):
        return pltpu.make_async_remote_copy(
            src_ref=source,
            dst_ref=target,
            send_sem=send,
            recv_sem=recv,
            device_id={"col": on_plane(k)},
            device_id_type=pl.DeviceIdType.MESH,
        )

    list_copies = []
    lists = ((rows_hbm, rows_list), (nodes_hbm, nodes_list), (counts_hbm, counts), (weights_hbm, weights))
    for i, (source, target) in enumerate(lists):
        list_copies.append(pltpu.make_async_copy(source, target, list_sem.at[i]))
        list_copies[-1].start()
    shape_copies = []
    for p in range(pieces):
        span = pl.ds(p * piece, piece)
        shape_copies.append(
            pltpu.make_async_copy(panels.at[0, span], shapes.at[span], local_sem.at[p])
        )
        shape_copies[-1].start()
    own_copies = []
    for q in range(chunks):
        own_copies.append(
            pltpu.make_async_copy(
                aic.at[pl.ds(q * sub, sub), pl.ds(pl.multiple_of(b * depth, depth), depth)],
                influence.at[q, b],
                local_sem.at[pieces + q],
            )
        )
        own_copies[-1].start()
    dof_span = pl.ds(lax.rem(c, senders) * share, share)
    own_modes = pltpu.make_async_copy(
        node_modes.at[dof_span], mode_rows.at[dof_span, b], local_sem.at[pieces + chunks]
    )

    barrier = pltpu.get_barrier_semaphore()
    for k in range(1, blocks):
        pl.semaphore_signal(
            barrier, inc=1, device_id={"blk": on_line(k)}, device_id_type=pl.DeviceIdType.MESH
        )
    for k in range(1, cols):
        pl.semaphore_signal(
            barrier, inc=1, device_id={"col": on_plane(k)}, device_id_type=pl.DeviceIdType.MESH
        )
    pl.semaphore_wait(barrier, blocks + cols - 2)

    aic_out = {}

    def send_rows(q):
        for k in range(1, blocks):
            peer = on_line(k)
            copy = to_line(
                k,
                aic.at[pl.ds(q * sub, sub), pl.ds(pl.multiple_of(peer * depth, depth), depth)],
                influence.at[q, b],
                aic_send.at[q, k - 1],
                aic_recv.at[q, k - 1],
            )
            copy.start()
            aic_out[q, k] = copy

    ahead = min(4, chunks)
    for q in range(ahead):
        send_rows(q)
        if q == 0:
            mode_out = [
                to_line(
                    k,
                    node_modes.at[dof_span],
                    mode_rows.at[dof_span, b],
                    mode_send.at[k - 1],
                    mode_recv.at[k - 1],
                )
                for k in range(1, blocks)
            ]

            @pl.when(c < senders)
            def _():
                own_modes.start()
                for copy in mode_out:
                    copy.start()

            length = dofs * owners * node_count
            row_at = lax.broadcasted_iota(jnp.int32, (sub, length), 0)
            column_at = lax.broadcasted_iota(jnp.int32, (sub, length), 1)
            total = jnp.zeros((sub, length), jnp.float32)
            for copy in list_copies:
                copy.wait()
            for o in range(owners):
                for s in range(slots):
                    live = s < counts[0, 0, o]
                    row = jnp.where(live, rows_list[0, 0, o, s], -1)
                    node = nodes_list[0, 0, o, s] + o * node_count
                    spread = jnp.zeros((sub, length), jnp.float32)
                    for d in range(dofs):
                        spread = jnp.where(
                            column_at == node + d * owners * node_count,
                            weights[0, 0, d, o, s],
                            spread,
                        )
                    total = total + jnp.where(row_at == row, spread, 0.0)
            spline[c, b] = total
            spline_out = []
            for k in range(1, blocks):
                copy = to_line(
                    k,
                    spline.at[c, b],
                    spline.at[c, b],
                    spline_send.at[k - 1],
                    spline_recv.at[k - 1],
                )
                copy.start()
                spline_out.append(copy)

    for p in range(pieces):
        shape_copies[p].wait()
        span = pl.ds(p * piece, piece)
        high, low = split(shapes[span])
        shapes_high[span] = high
        shapes_low[span] = low

    for copy in spline_out:
        copy.wait()
    for k in range(1, cols):
        copy = to_plane(
            k,
            spline.at[c],
            spline.at[c],
            spline_send.at[blocks - 2 + k],
            spline_recv.at[blocks - 2 + k],
        )
        copy.start()
        spline_out.append(copy)
    mode_plane = [
        to_plane(
            k,
            mode_rows.at[dof_span],
            mode_rows.at[dof_span],
            mode_send.at[blocks - 2 + k],
            mode_recv.at[blocks - 2 + k],
        )
        for k in range(1, cols)
    ]

    @pl.when(c < senders)
    def _():
        own_modes.wait()
        for copy in mode_out:
            copy.wait()
        for copy in mode_plane:
            copy.start()

    plane_out, line_out, final_out = {}, {}, {}

    def await_rows(q):
        own_copies[q].wait()
        for k in range(1, blocks):
            aic_out[q, k].wait_recv()

    def multiply(q):
        high, low = split(influence[q].reshape(blocks * sub, depth))
        product = jnp.dot(
            jnp.concatenate([high, low], axis=0),
            shapes_high[...],
            preferred_element_type=jnp.float32,
        )
        rest = jnp.dot(high, shapes_low[...], preferred_element_type=jnp.float32)
        lines = blocks * sub
        product = product[:lines] + (product[lines:] + rest)
        partial[q] = product.reshape(blocks, sub, width)
        for k in range(1, cols):
            copy = to_plane(
                k,
                partial.at[q, on_plane(k)],
                plane_in.at[q, k - 1],
                plane_send.at[q, k - 1],
                plane_recv.at[q, k - 1],
            )
            copy.start()
            plane_out[q, k] = copy

    def over_plane(q):
        total = partial[q, c]
        for k in range(1, cols):
            plane_out[q, k].wait_recv()
            total = total + plane_in[q, k - 1]
        line_in[q, b] = total
        for k in range(1, blocks):
            copy = to_line(
                k,
                line_in.at[q, b],
                line_in.at[q, b],
                line_send.at[q, k - 1],
                line_recv.at[q, k - 1],
            )
            copy.start()
            line_out[q, k] = copy

    def over_line(q):
        for k in range(1, blocks):
            line_out[q, k].wait_recv()
        total = line_in[q, 0]
        for source in range(1, blocks):
            total = total + line_in[q, source]
        pressure[q, c] = total
        for k in range(1, cols):
            copy = to_plane(
                k,
                pressure.at[q, c],
                pressure.at[q, c],
                final_send.at[q, k - 1],
                final_recv.at[q, k - 1],
            )
            copy.start()
            final_out[q, k] = copy

    def make_force():
        for k in range(1, cols):
            spline_out[blocks - 2 + k].wait_recv()

            @pl.when(lax.rem(c + cols - k, cols) < senders)
            def _():
                mode_plane[k - 1].wait_recv()

        length = dofs * owners * node_count
        force[...] = jnp.dot(
            spline[...].reshape(cols * blocks * sub, length),
            mode_rows[...].reshape(length, modes),
            precision=HIGHEST,
            preferred_element_type=jnp.float32,
        )

    def modal(start, stop):
        force_rows = force[pl.ds(start * blocks * sub, (stop - start) * blocks * sub)]
        return lax.dot_general(
            force_rows,
            pressure[start:stop].reshape((stop - start) * blocks * sub, width),
            (((0,), (0,)), ((), ())),
            precision=HIGHEST,
            preferred_element_type=jnp.float32,
        )

    def await_pressure(q):
        for k in range(1, cols):
            final_out[q, k].wait_recv()

    for q in range(chunks):
        await_rows(q)
        if q + ahead < chunks:
            send_rows(q + ahead)
        multiply(q)
        if q == chunks - 1:
            for earlier in range(q):
                over_plane(earlier)
        if q == 1:
            make_force()
    last = chunks - 1
    over_plane(last)
    for q in range(chunks):
        over_line(q)
    if last:
        for q in range(last):
            await_pressure(q)
        out[...] = modal(0, last)
        await_pressure(last)
        out[...] += modal(last, chunks)
    else:
        await_pressure(last)
        out[...] = modal(last, chunks)

    for copy in spline_out[blocks - 1 :]:
        copy.wait_send()
    for group in (aic_out, plane_out, line_out, final_out):
        for copy in group.values():
            copy.wait_send()

    @pl.when(c < senders)
    def _():
        for copy in mode_plane:
            copy.wait_send()


def by_kernel(aic, downwash, node_modes, src_rows, dst_nodes, counts, spline_weights):
    blocks = lax.axis_size("blk")
    cols = lax.axis_size("col")
    rows = aic.shape[0]
    sub = rows // cols
    depth, width = downwash.shape[1:]
    dofs, node_count, modes = node_modes.shape
    length = dofs * blocks * node_count
    pieces = 4
    dma = pltpu.SemaphoreType.DMA
    anywhere = pl.BlockSpec(memory_space=pl.ANY)
    return pl.pallas_call(
        functools.partial(exchange_kernel, blocks, cols),
        name="gaf_exchange",
        out_shape=jax.ShapeDtypeStruct((modes, width), jnp.float32),
        in_specs=[anywhere] * 7,
        out_specs=pl.BlockSpec(memory_space=pltpu.VMEM),
        scratch_shapes=[
            pltpu.VMEM((cols, blocks, sub, depth), jnp.float32),
            pltpu.VMEM((depth, width), jnp.float32),
            pltpu.VMEM((depth, width), jnp.bfloat16),
            pltpu.VMEM((depth, width), jnp.bfloat16),
            pltpu.VMEM((cols, blocks, sub, width), jnp.float32),
            pltpu.VMEM((cols, cols - 1, sub, width), jnp.float32),
            pltpu.VMEM((cols, blocks, sub, width), jnp.float32),
            pltpu.VMEM((cols, blocks, sub, width), jnp.float32),
            pltpu.VMEM((cols, blocks, sub, length), jnp.float32),
            pltpu.VMEM((dofs, blocks, node_count, modes), jnp.float32),
            pltpu.VMEM((cols * blocks * sub, modes), jnp.float32),
            pltpu.SMEM(src_rows.shape, jnp.int32),
            pltpu.SMEM(dst_nodes.shape, jnp.int32),
            pltpu.SMEM(counts.shape, jnp.int32),
            pltpu.SMEM(spline_weights.shape, jnp.float32),
            dma((4,)),
            dma((pieces + cols + 1,)),
            dma((cols, blocks - 1)),
            dma((cols, blocks - 1)),
            dma((cols, cols - 1)),
            dma((cols, cols - 1)),
            dma((cols, blocks - 1)),
            dma((cols, blocks - 1)),
            dma((cols, cols - 1)),
            dma((cols, cols - 1)),
            dma((blocks + cols - 2,)),
            dma((blocks + cols - 2,)),
            dma((blocks + cols - 2,)),
            dma((blocks + cols - 2,)),
        ],
        compiler_params=pltpu.CompilerParams(
            collective_id=0, has_side_effects=True, vmem_limit_bytes=60 * 1024 * 1024
        ),
    )(aic, downwash, node_modes, src_rows, dst_nodes, counts, spline_weights)


def solution(mesh):
    placed = (
        P(("groups", "blk"), "col"),
        P(("groups", "col"), "blk", None),
        P(None, "blk", None),
        P("blk", "col", None, None),
        P("blk", "col", None, None),
        P("blk", "col", None),
        P("blk", "col", None, None, None),
    )

    def shards(*operands):
        aic, downwash, node_modes = operands[:3]
        blocks, cols = lax.axis_size("blk"), lax.axis_size("col")
        small = blocks * aic.shape[0] <= 2 * node_modes.shape[2]
        even = blocks == cols and aic.shape[0] % (8 * cols) == 0 and downwash.shape[1] % 512 == 0
        if small and even:
            return by_kernel(*operands)
        return by_rotation(*operands)

    return jax.shard_map(
        shards, mesh=mesh, in_specs=placed, out_specs=P("groups", None), check_vma=False
    )
```

```python
import functools

import jax
import jax.numpy as jnp
from jax import lax
from jax.experimental import pallas as pl
from jax.experimental.pallas import tpu as pltpu
from jax.sharding import PartitionSpec as P


HIGHEST = lax.Precision.HIGHEST


def shifted(value, axis, steps):
    count = lax.axis_size(axis)
    pairs = [(source, (source + steps) % count) for source in range(count)]
    return lax.ppermute(value, axis, pairs)


def by_rotation(aic, downwash, node_modes, src_rows, dst_nodes, counts, spline_weights):
    cycle_size = lax.axis_size("blk")
    col_count = lax.axis_size("col")
    device = lax.axis_index("blk")
    own_block = downwash[0]
    panel_rows = own_block.shape[0]

    def product(shapes, source):
        columns = lax.dynamic_slice_in_dim(aic, source * panel_rows, panel_rows, 1)
        return jnp.dot(
            columns, shapes, precision=lax.Precision.HIGHEST, preferred_element_type=jnp.float32
        )

    halfway = cycle_size // 2

    def advance(offset, running):
        pressure, forward, behind = running
        forward = shifted(forward, "blk", 1)
        behind = shifted(behind, "blk", -1)
        pressure = pressure + product(forward, (device - offset) % cycle_size)
        pressure = pressure + product(behind, (device + offset) % cycle_size)
        return (pressure, forward, behind)

    pressure = product(own_block, device)
    pressure, forward, behind = lax.fori_loop(1, halfway, advance, (pressure, own_block, own_block))
    forward = shifted(forward, "blk", 1)
    pressure = pressure + product(forward, (device - halfway) % cycle_size)
    slots = src_rows.shape[-1]
    slot_index = jnp.arange(slots, dtype=jnp.int32)
    all_rows, all_nodes, all_counts = (
        lax.all_gather(src_rows, "col", axis=1, tiled=True),
        lax.all_gather(dst_nodes, "col", axis=1, tiled=True),
        lax.all_gather(counts, "col", axis=1, tiled=True),
    )
    weight_all = lax.all_gather(spline_weights, "col", axis=1, tiled=True)
    sub_rows = pressure.shape[0] // col_count
    offsets = jnp.arange(col_count, dtype=jnp.int32)[:, None, None] * sub_rows
    shifted_rows = all_rows[0] + offsets
    row_ids = jnp.transpose(shifted_rows, (1, 0, 2)).reshape(cycle_size, col_count * slots)
    node_ids = jnp.transpose(all_nodes[0], (1, 0, 2)).reshape(cycle_size, col_count * slots)
    live_sub = (slot_index[None, None, :] < all_counts[0][:, :, None]).astype(jnp.float32)
    live = jnp.transpose(live_sub, (1, 0, 2)).reshape(cycle_size, col_count * slots)
    weight_rows = jnp.transpose(weight_all[0], (1, 2, 0, 3)).reshape(
        6, cycle_size, col_count * slots
    )
    node_count = node_modes.shape[1]
    forces = pressure[row_ids.T]
    picks = (node_ids[None, :, :] == jnp.arange(node_count, dtype=jnp.int32)[:, None, None]).astype(
        jnp.float32
    )
    spread = weight_rows[:, None, :, :] * live[None, None, :, :] * picks[None, :, :, :]
    spread = spread.reshape(6 * node_count, cycle_size, row_ids.shape[1])
    arrived_forces, arrived_spread = (
        lax.all_to_all(forces, "blk", split_axis=1, concat_axis=1, tiled=True),
        lax.all_to_all(spread, "blk", split_axis=1, concat_axis=1, tiled=True),
    )
    loads = jnp.einsum(
        "jsc,csk->jk", arrived_spread, arrived_forces, precision=lax.Precision.HIGHEST
    )
    flat_modes = node_modes.reshape(6 * node_count, node_modes.shape[2])
    modal = jnp.einsum("jm,jk->mk", flat_modes, loads, precision=lax.Precision.HIGHEST)
    return lax.psum(modal, ("blk", "col"))


def split(value):
    high = value.astype(jnp.bfloat16)
    low = (value - high.astype(jnp.float32)).astype(jnp.bfloat16)
    return high, low


def exchange_kernel(
    blocks,
    cols,
    aic,
    panels,
    node_modes,
    rows_hbm,
    nodes_hbm,
    counts_hbm,
    weights_hbm,
    out,
    influence,
    shapes,
    shapes_high,
    shapes_low,
    partial,
    plane_in,
    line_in,
    pressure,
    spline,
    mode_rows,
    force,
    rows_list,
    nodes_list,
    counts,
    weights,
    list_sem,
    local_sem,
    aic_send,
    aic_recv,
    plane_send,
    plane_recv,
    line_send,
    line_recv,
    final_send,
    final_recv,
    spline_send,
    spline_recv,
    mode_send,
    mode_recv,
):
    b = lax.axis_index("blk")
    c = lax.axis_index("col")
    chunks, _, sub, depth = influence.shape
    dofs, _, node_count, modes = mode_rows.shape
    owners, slots = rows_list.shape[2:]
    width = panels.shape[2]
    senders = min(cols, dofs)
    while dofs % senders:
        senders -= 1
    share = dofs // senders
    pieces = local_sem.shape[0] - chunks - 1
    piece = depth // pieces

    def on_line(k):
        return lax.rem(b + k, blocks)

    def on_plane(k):
        return lax.rem(c + k, cols)

    def to_line(k, source, target, send, recv):
        return pltpu.make_async_remote_copy(
            src_ref=source,
            dst_ref=target,
            send_sem=send,
            recv_sem=recv,
            device_id={"blk": on_line(k)},
            device_id_type=pl.DeviceIdType.MESH,
        )

    def to_plane(k, source, target, send, recv):
        return pltpu.make_async_remote_copy(
            src_ref=source,
            dst_ref=target,
            send_sem=send,
            recv_sem=recv,
            device_id={"col": on_plane(k)},
            device_id_type=pl.DeviceIdType.MESH,
        )

    list_copies = []
    lists = ((rows_hbm, rows_list), (nodes_hbm, nodes_list), (counts_hbm, counts), (weights_hbm, weights))
    for i, (source, target) in enumerate(lists):
        list_copies.append(pltpu.make_async_copy(source, target, list_sem.at[i]))
        list_copies[-1].start()
    shape_copies = []
    for p in range(pieces):
        span = pl.ds(p * piece, piece)
        shape_copies.append(
            pltpu.make_async_copy(panels.at[0, span], shapes.at[span], local_sem.at[p])
        )
        shape_copies[-1].start()
    own_copies = []
    for q in range(chunks):
        own_copies.append(
            pltpu.make_async_copy(
                aic.at[pl.ds(q * sub, sub), pl.ds(pl.multiple_of(b * depth, depth), depth)],
                influence.at[q, b],
                local_sem.at[pieces + q],
            )
        )
        own_copies[-1].start()
    dof_span = pl.ds(lax.rem(c, senders) * share, share)
    own_modes = pltpu.make_async_copy(
        node_modes.at[dof_span], mode_rows.at[dof_span, b], local_sem.at[pieces + chunks]
    )

    barrier = pltpu.get_barrier_semaphore()
    for k in range(1, blocks):
        pl.semaphore_signal(
            barrier, inc=1, device_id={"blk": on_line(k)}, device_id_type=pl.DeviceIdType.MESH
        )
    for k in range(1, cols):
        pl.semaphore_signal(
            barrier, inc=1, device_id={"col": on_plane(k)}, device_id_type=pl.DeviceIdType.MESH
        )
    pl.semaphore_wait(barrier, blocks + cols - 2)

    aic_out = {}

    def send_rows(q):
        for k in range(1, blocks):
            peer = on_line(k)
            copy = to_line(
                k,
                aic.at[pl.ds(q * sub, sub), pl.ds(pl.multiple_of(peer * depth, depth), depth)],
                influence.at[q, b],
                aic_send.at[q, k - 1],
                aic_recv.at[q, k - 1],
            )
            copy.start()
            aic_out[q, k] = copy

    ahead = min(4, chunks)
    for q in range(ahead):
        send_rows(q)
        if q == 0:
            mode_out = [
                to_line(
                    k,
                    node_modes.at[dof_span],
                    mode_rows.at[dof_span, b],
                    mode_send.at[k - 1],
                    mode_recv.at[k - 1],
                )
                for k in range(1, blocks)
            ]

            @pl.when(c < senders)
            def _():
                own_modes.start()
                for copy in mode_out:
                    copy.start()

            length = dofs * owners * node_count
            row_at = lax.broadcasted_iota(jnp.int32, (sub, length), 0)
            column_at = lax.broadcasted_iota(jnp.int32, (sub, length), 1)
            total = jnp.zeros((sub, length), jnp.float32)
            for copy in list_copies:
                copy.wait()
            for o in range(owners):
                for s in range(slots):
                    live = s < counts[0, 0, o]
                    row = jnp.where(live, rows_list[0, 0, o, s], -1)
                    node = nodes_list[0, 0, o, s] + o * node_count
                    spread = jnp.zeros((sub, length), jnp.float32)
                    for d in range(dofs):
                        spread = jnp.where(
                            column_at == node + d * owners * node_count,
                            weights[0, 0, d, o, s],
                            spread,
                        )
                    total = total + jnp.where(row_at == row, spread, 0.0)
            spline[c, b] = total
            spline_out = []
            for k in range(1, blocks):
                copy = to_line(
                    k,
                    spline.at[c, b],
                    spline.at[c, b],
                    spline_send.at[k - 1],
                    spline_recv.at[k - 1],
                )
                copy.start()
                spline_out.append(copy)

    for p in range(pieces):
        shape_copies[p].wait()
        span = pl.ds(p * piece, piece)
        high, low = split(shapes[span])
        shapes_high[span] = high
        shapes_low[span] = low

    for copy in spline_out:
        copy.wait()
    for k in range(1, cols):
        copy = to_plane(
            k,
            spline.at[c],
            spline.at[c],
            spline_send.at[blocks - 2 + k],
            spline_recv.at[blocks - 2 + k],
        )
        copy.start()
        spline_out.append(copy)
    mode_plane = [
        to_plane(
            k,
            mode_rows.at[dof_span],
            mode_rows.at[dof_span],
            mode_send.at[blocks - 2 + k],
            mode_recv.at[blocks - 2 + k],
        )
        for k in range(1, cols)
    ]

    @pl.when(c < senders)
    def _():
        own_modes.wait()
        for copy in mode_out:
            copy.wait()
        for copy in mode_plane:
            copy.start()

    plane_out, line_out, final_out = {}, {}, {}

    def await_rows(q):
        own_copies[q].wait()
        for k in range(1, blocks):
            aic_out[q, k].wait_recv()

    def multiply(q):
        high, low = split(influence[q].reshape(blocks * sub, depth))
        product = jnp.dot(
            jnp.concatenate([high, low], axis=0),
            shapes_high[...],
            preferred_element_type=jnp.float32,
        )
        rest = jnp.dot(high, shapes_low[...], preferred_element_type=jnp.float32)
        lines = blocks * sub
        product = product[:lines] + (product[lines:] + rest)
        partial[q] = product.reshape(blocks, sub, width)
        for k in range(1, cols):
            copy = to_plane(
                k,
                partial.at[q, on_plane(k)],
                plane_in.at[q, k - 1],
                plane_send.at[q, k - 1],
                plane_recv.at[q, k - 1],
            )
            copy.start()
            plane_out[q, k] = copy

    def over_plane(q):
        total = partial[q, c]
        for k in range(1, cols):
            plane_out[q, k].wait_recv()
            total = total + plane_in[q, k - 1]
        line_in[q, b] = total
        for k in range(1, blocks):
            copy = to_line(
                k,
                line_in.at[q, b],
                line_in.at[q, b],
                line_send.at[q, k - 1],
                line_recv.at[q, k - 1],
            )
            copy.start()
            line_out[q, k] = copy

    def over_line(q):
        for k in range(1, blocks):
            line_out[q, k].wait_recv()
        total = line_in[q, 0]
        for source in range(1, blocks):
            total = total + line_in[q, source]
        pressure[q, c] = total
        for k in range(1, cols):
            copy = to_plane(
                k,
                pressure.at[q, c],
                pressure.at[q, c],
                final_send.at[q, k - 1],
                final_recv.at[q, k - 1],
            )
            copy.start()
            final_out[q, k] = copy

    def make_force():
        for k in range(1, cols):
            spline_out[blocks - 2 + k].wait_recv()

            @pl.when(lax.rem(c + cols - k, cols) < senders)
            def _():
                mode_plane[k - 1].wait_recv()

        length = dofs * owners * node_count
        force[...] = jnp.dot(
            spline[...].reshape(cols * blocks * sub, length),
            mode_rows[...].reshape(length, modes),
            precision=HIGHEST,
            preferred_element_type=jnp.float32,
        )

    def modal(start, stop):
        force_rows = force[pl.ds(start * blocks * sub, (stop - start) * blocks * sub)]
        return lax.dot_general(
            force_rows,
            pressure[start:stop].reshape((stop - start) * blocks * sub, width),
            (((0,), (0,)), ((), ())),
            precision=HIGHEST,
            preferred_element_type=jnp.float32,
        )

    def await_pressure(q):
        for k in range(1, cols):
            final_out[q, k].wait_recv()

    for q in range(chunks):
        await_rows(q)
        if q + ahead < chunks:
            send_rows(q + ahead)
        multiply(q)
        if q == chunks - 1:
            for earlier in range(q):
                over_plane(earlier)
        if q == 1:
            make_force()
    last = chunks - 1
    over_plane(last)
    for q in range(chunks):
        over_line(q)
    if last:
        for q in range(last):
            await_pressure(q)
        out[...] = modal(0, last)
        await_pressure(last)
        out[...] += modal(last, chunks)
    else:
        await_pressure(last)
        out[...] = modal(last, chunks)

    for copy in spline_out[blocks - 1 :]:
        copy.wait_send()
    for group in (aic_out, plane_out, line_out, final_out):
        for copy in group.values():
            copy.wait_send()

    @pl.when(c < senders)
    def _():
        for copy in mode_plane:
            copy.wait_send()


def by_kernel(aic, downwash, node_modes, src_rows, dst_nodes, counts, spline_weights):
    blocks = lax.axis_size("blk")
    cols = lax.axis_size("col")
    rows = aic.shape[0]
    sub = rows // cols
    depth, width = downwash.shape[1:]
    dofs, node_count, modes = node_modes.shape
    length = dofs * blocks * node_count
    pieces = 4
    dma = pltpu.SemaphoreType.DMA
    anywhere = pl.BlockSpec(memory_space=pl.ANY)
    return pl.pallas_call(
        functools.partial(exchange_kernel, blocks, cols),
        name="gaf_exchange",
        out_shape=jax.ShapeDtypeStruct((modes, width), jnp.float32),
        in_specs=[anywhere] * 7,
        out_specs=pl.BlockSpec(memory_space=pltpu.VMEM),
        scratch_shapes=[
            pltpu.VMEM((cols, blocks, sub, depth), jnp.float32),
            pltpu.VMEM((depth, width), jnp.float32),
            pltpu.VMEM((depth, width), jnp.bfloat16),
            pltpu.VMEM((depth, width), jnp.bfloat16),
            pltpu.VMEM((cols, blocks, sub, width), jnp.float32),
            pltpu.VMEM((cols, cols - 1, sub, width), jnp.float32),
            pltpu.VMEM((cols, blocks, sub, width), jnp.float32),
            pltpu.VMEM((cols, blocks, sub, width), jnp.float32),
            pltpu.VMEM((cols, blocks, sub, length), jnp.float32),
            pltpu.VMEM((dofs, blocks, node_count, modes), jnp.float32),
            pltpu.VMEM((cols * blocks * sub, modes), jnp.float32),
            pltpu.SMEM(src_rows.shape, jnp.int32),
            pltpu.SMEM(dst_nodes.shape, jnp.int32),
            pltpu.SMEM(counts.shape, jnp.int32),
            pltpu.SMEM(spline_weights.shape, jnp.float32),
            dma((4,)),
            dma((pieces + cols + 1,)),
            dma((cols, blocks - 1)),
            dma((cols, blocks - 1)),
            dma((cols, cols - 1)),
            dma((cols, cols - 1)),
            dma((cols, blocks - 1)),
            dma((cols, blocks - 1)),
            dma((cols, cols - 1)),
            dma((cols, cols - 1)),
            dma((blocks + cols - 2,)),
            dma((blocks + cols - 2,)),
            dma((blocks + cols - 2,)),
            dma((blocks + cols - 2,)),
        ],
        compiler_params=pltpu.CompilerParams(
            collective_id=0, has_side_effects=True, vmem_limit_bytes=54200 * 1024
        ),
    )(aic, downwash, node_modes, src_rows, dst_nodes, counts, spline_weights)


def solution(mesh):
    placed = (
        P(("groups", "blk"), "col"),
        P(("groups", "col"), "blk", None),
        P(None, "blk", None),
        P("blk", "col", None, None),
        P("blk", "col", None, None),
        P("blk", "col", None),
        P("blk", "col", None, None, None),
    )

    def shards(*operands):
        aic, downwash, node_modes = operands[:3]
        blocks, cols = lax.axis_size("blk"), lax.axis_size("col")
        small = blocks * aic.shape[0] <= 2 * node_modes.shape[2]
        even = blocks == cols and aic.shape[0] % (8 * cols) == 0 and downwash.shape[1] % 512 == 0
        if small and even:
            return by_kernel(*operands)
        return by_rotation(*operands)

    return jax.shard_map(
        shards, mesh=mesh, in_specs=placed, out_specs=P("groups", None), check_vma=False
    )
```
